32 devices in a mesh: row: 4 (over z), col: 8 (over y, x, core).
Axes of the slice: x: 2, y: 2, z: 4, core: 2. Of those that a mesh axis runs over, the one named last changes fastest.
Arguments:
- scans: float32 [4096, 4, 8, 128], P(('row', 'col')), may hold values from -6 to 6
- dest: int32 [4096, 1], P(('row', 'col')), may hold values from 0 to 31; in each aligned block of 128 rows (0 to 127, 128 to 255, ...) at most 8 rows name the same one
- offsets: int32 [4096], P(('row', 'col')), may hold values from 0 to 252
- profile_index: int32 [4096], P(('row', 'col')), may hold values from 0 to 15
- profiles: float32 [16, 4, 128], replicated, may hold values from 0.1 to 1.5
- embed_weight: bfloat16 [512, 1024], replicated, may hold values from -0.25 to 0.25
- attn_gain: float32 [2, 1024], replicated, may hold values from 0.1 to 1.9
- qkv_weight: bfloat16 [2, 1024, 3072], replicated, may hold values from -3 to 3
- out_weight: bfloat16 [2, 1024, 1024], replicated, may hold values from -0.1875 to 0.1875
Outputs:
- tokens: bfloat16 [128, 128, 1024], P('row', 'col')
The draws below stay inside these ranges and needn't reach their ends.
Inputs may be any that keep to these rules, and one draw needn't show every extreme that they name: dest[b, 0] is the tile of block b, numbered 8 * tile row + tile column; of the 128 blocks of one device at most 8 go to any one tile.
All inputs are finite; a program needn't handle non-finite values.
Results may differ from the reference program's by a relative error of at most 0.012.
Values may be sent and summed in bfloat16 or wider, within the bound.
A program may use at most 128 MiB of HBM per device.

```python
import math
import jax
import jax.numpy as jnp
import numpy as np
from jax import lax

C = 8
D = 1024
HEADS = 16
RADIUS = 4
LAYERS = 2
BR = 4
NWT = 16
TOK_H = 32
TOK_W = 16
SCANS = 128
CAP = 8
NBLK = 4096
N_ROW = 4
N_COL = 8
DEVICES = 32


def draw_qkv_weight(key, part):
    drawn = jnp.clip(jax.random.normal(key, (LAYERS, D, 3 * D), jnp.float32), -4.0, 4.0) * D ** (-0.5)
    return drawn.astype(jnp.bfloat16)


def plant(entries, own_key, smallest, high):
    spot = [jax.random.randint(jax.random.fold_in(own_key, axis), (), 0, length) for axis, length in enumerate(entries.shape)]
    longest = entries.shape.index(max(entries.shape))
    neighbour = spot[:longest] + [(spot[longest] + 1) % entries.shape[longest]] + spot[longest + 1:]
    return entries.at[tuple(spot)].set(smallest).at[tuple(neighbour)].set(high)


def block_levels(stream_key, shape, cuts, smallest, top_value):
    loudness, own = 1.0, jax.random.fold_in(stream_key, 6)
    for dim, parts in cuts:
        steps = jnp.exp(jax.random.uniform(jax.random.fold_in(own, dim), (parts,), jnp.float32, smallest / len(cuts), top_value / len(cuts)))
        loudness = loudness * jnp.repeat(steps, shape[dim] // parts).reshape([-1 if axis == dim else 1 for axis in range(len(shape))])
    return loudness


def routed_block(own_key, own, number, rows, amount, top, bound, skew):
    ranking = jax.random.permutation(own_key, amount)
    heavy_load, common = portions_of(amount, rows * top, bound, skew, True), portions_of(amount, rows * top, bound, skew, False)
    places = jnp.arange(amount)

    def named(lengths, rotation):
        used = int((lengths > 0).sum())
        fixed = max(1, used // 4)
        moved = fixed + (places - fixed + rotation * (used - fixed)) % max(1, amount - fixed)
        return jnp.zeros((amount,), jnp.int32).at[ranking[jnp.where(places < fixed, places, moved)]].set(jnp.asarray(lengths, jnp.int32))

    lengths = jnp.where(number % 4 == 0, named(heavy_load, number // 4), named(common, number - number // 4 - 1))
    mixed = jax.random.permutation(jax.random.fold_in(own, 3), amount)
    giver, taker = mixed[0:amount // 2 * 2:2], mixed[1:amount // 2 * 2:2]
    slack = jnp.minimum(lengths[giver] - 1, bound - lengths[taker]) // 2
    slack = jnp.where((giver == ranking[0]) | (taker == ranking[0]) | (lengths[taker] == 0), 0, jnp.maximum(slack, 0))
    moved = jax.random.randint(jax.random.fold_in(own, 4), (amount // 2,), 0, 1 << 20) % (slack + 1)
    lengths = lengths.at[giver].add(-moved).at[taker].add(moved)
    items = jnp.searchsorted(jnp.cumsum(lengths), jnp.arange(rows * top), side="right").astype(jnp.int32)
    table = items.reshape(top, rows).T
    table = table[jax.random.permutation(jax.random.fold_in(own, 1), rows)]
    rotation = jax.random.randint(jax.random.fold_in(own, 2), (rows, 1), 0, top)
    return jnp.take_along_axis(table, (jnp.arange(top)[None, :] + rotation) % top, axis=1)


def portions_of(number_of, total, limit, slope, full):
    weights = [(1 << 20) // math.isqrt(grade ** slope) + 1 for grade in range(1, number_of + 1)]
    largest = limit if full else min(limit, max(-(-total // number_of), total * weights[0] // sum(weights)))
    least = 1 if total - largest >= number_of - 1 else 0
    holding, surplus = [largest] + [least] * (number_of - 1), total - largest - least * (number_of - 1)
    while surplus > 0:
        movable = [i for i in range(1, number_of) if holding[i] < largest] or [i for i in range(1, number_of) if holding[i] < limit]
        pool, budget = sum([weights[i] for i in movable]), surplus
        for i in movable:
            extra = min(limit - holding[i], max(1, budget * weights[i] // pool), surplus)
            holding[i] = holding[i] + extra
            surplus = surplus - extra
    return np.array(holding)


def noise(stream_key, shape, deviation, most, pieces=(), kind=jnp.bfloat16):
    array = jax.random.normal(stream_key, shape, jnp.float32) * deviation
    if len(pieces) > 0:
        array = block_levels(stream_key, shape, pieces, -0.22, 0.18) * array
    return jnp.clip(array, min=-most, max=most).astype(kind)


def setup_inputs(seed: int = 0) -> dict:
    arg_keys = jax.random.split(jax.random.key(seed), 10)
    scans = noise(arg_keys[0], (NBLK, BR, C, 8 * TOK_W), 1.0, 6.0, ((0, 32),), jnp.float32)
    dest_keys = jax.random.split(jax.random.fold_in(arg_keys[1], 1), NBLK // SCANS)
    dest_turns = jax.random.permutation(jax.random.fold_in(arg_keys[1], 3), NBLK // SCANS)
    dest = jax.vmap(lambda own, number: routed_block(jax.random.fold_in(arg_keys[1], 2), own, number, SCANS, DEVICES, 1, CAP, 2))(dest_keys, dest_turns).reshape((NBLK, 1))
    offsets = plant(jax.random.randint(arg_keys[2], (NBLK,), 0, 8 * TOK_H - BR + 1), jax.random.fold_in(arg_keys[2], 1), 0, 8 * TOK_H - BR).astype(jnp.int32)
    profile_index = plant(jax.random.randint(arg_keys[3], (NBLK,), 0, NWT), jax.random.fold_in(arg_keys[3], 1), 0, NWT - 1).astype(jnp.int32)
    profiles = jnp.clip(jnp.exp(jax.random.uniform(arg_keys[4], (NWT, BR, 8 * TOK_W), jnp.float32, math.log(0.1), math.log(1.5))), 0.1, 1.5)
    embed_weight = noise(arg_keys[5], (64 * C, D), (64 * C) ** -0.5, 0.25)
    attn_gain = jnp.clip(1.0 + 0.18 * jax.random.normal(arg_keys[6], (LAYERS, D), jnp.float32), 0.1, 1.9)
    qkv_weight = draw_qkv_weight(jax.random.fold_in(arg_keys[9], 71), 0)
    out_weight = noise(arg_keys[8], (LAYERS, D, D), D ** -0.5, 0.1875)
    return dict(scans=scans, dest=dest, offsets=offsets, profile_index=profile_index, profiles=profiles, embed_weight=embed_weight, attn_gain=attn_gain, qkv_weight=qkv_weight, out_weight=out_weight)


def normed(stream, gain_row):
    centre = lax.optimization_barrier(jnp.mean(stream, -1, keepdims=True))
    spread = lax.optimization_barrier(jnp.mean(jnp.square(stream - centre), -1, keepdims=True))
    return ((stream - centre) * lax.rsqrt(spread + 1e-05) * gain_row).astype(jnp.bfloat16)

def reference(scans, dest, offsets, profile_index, profiles, embed_weight, attn_gain, qkv_weight, out_weight):
    tile_rows = TOK_H * 8
    tile_cols = TOK_W * 8
    grid_h = TOK_H * N_ROW
    grid_w = TOK_W * N_COL
    pixel_cols = grid_w * 8
    pixel_total = grid_h * 8 * pixel_cols
    targets = dest[:, 0]
    block_weight = profiles[profile_index]
    weighted = scans * block_weight[:, :, None, :]
    top_row = (targets // N_COL * tile_rows + offsets).astype(jnp.int32)
    left_col = (targets % N_COL * tile_cols).astype(jnp.int32)
    pix_rows = top_row[:, None] + jnp.arange(BR, dtype=jnp.int32)[None, :]
    pix_cols = left_col[:, None] + jnp.arange(tile_cols, dtype=jnp.int32)[None, :]
    flat_idx = (pix_rows[:, :, None] * pixel_cols + pix_cols[:, None, :]).reshape(-1).astype(jnp.int32)
    weighted_rows = weighted.transpose(0, 1, 3, 2).reshape(-1, C)
    numerator = jax.ops.segment_sum(weighted_rows, flat_idx, num_segments=pixel_total)
    numerator = numerator.reshape(grid_h * 8, pixel_cols, C).transpose(0, 2, 1)
    weight_sum = jax.ops.segment_sum(block_weight.reshape(-1), flat_idx, num_segments=pixel_total)
    weight_sum = weight_sum.reshape(grid_h * 8, pixel_cols)
    merged = (numerator / (1.0 + weight_sum[:, None, :])).astype(jnp.bfloat16)
    patches = merged.reshape(grid_h, 8, C, grid_w, 8).transpose(0, 3, 2, 1, 4).reshape(grid_h * grid_w, C * 64)
    stream = jnp.dot(patches, embed_weight, preferred_element_type=jnp.float32)
    head_dim = D // HEADS
    score_scale = head_dim ** (-0.5)
    window = 2 * RADIUS + 1
    inside_grid = jnp.pad(jnp.ones((grid_h, grid_w), jnp.float32), RADIUS)
    padding = ((RADIUS, RADIUS), (RADIUS, RADIUS), (0, 0), (0, 0))
    for layer_idx in range(LAYERS):
        inputs = normed(stream, attn_gain[layer_idx])
        projected = jnp.dot(inputs, qkv_weight[layer_idx], preferred_element_type=jnp.float32).astype(jnp.bfloat16)
        queries = projected[:, :D].reshape(grid_h, grid_w, HEADS, head_dim)
        key_heads = jnp.pad(projected[:, D:2 * D].reshape(grid_h, grid_w, HEADS, head_dim), padding)
        values = jnp.pad(projected[:, 2 * D:].reshape(grid_h, grid_w, HEADS, head_dim), padding)

        def one_row(row_idx):
            query_row = lax.dynamic_index_in_dim(queries, row_idx, 0, keepdims=False).astype(jnp.float32)
            key_slab = lax.dynamic_slice_in_dim(key_heads, row_idx, window, 0)
            value_slab = lax.dynamic_slice_in_dim(values, row_idx, window, 0)
            mask_slab = lax.dynamic_slice_in_dim(inside_grid, row_idx, window, 0)
            logit_list = []
            for row_step in range(window):
                for col_step in range(window):
                    shifted = key_slab[row_step, col_step:col_step + grid_w].astype(jnp.float32)
                    logits = lax.optimization_barrier(jnp.sum(query_row * shifted, -1)) * score_scale
                    inside = mask_slab[row_step, col_step:col_step + grid_w][:, None] > 0.5
                    logit_list.append(jnp.where(inside, logits, -1e+30))
            logits = jnp.stack(logit_list)
            row_max = lax.optimization_barrier(jnp.max(logits, 0))
            exponent = jnp.exp(logits - row_max)
            attention = (exponent / lax.optimization_barrier(jnp.sum(exponent, 0))).astype(jnp.bfloat16)
            accumulated = jnp.zeros((grid_w, HEADS, head_dim), jnp.float32)
            for row_step in range(window):
                for col_step in range(window):
                    shifted = value_slab[row_step, col_step:col_step + grid_w].astype(jnp.float32)
                    share = attention[row_step * window + col_step][:, :, None].astype(jnp.float32)
                    accumulated = accumulated + share * shifted
            return accumulated.astype(jnp.bfloat16)
        attended = lax.map(one_row, jnp.arange(grid_h, dtype=jnp.int32)).reshape(grid_h * grid_w, D)
        stream = stream + jnp.dot(attended, out_weight[layer_idx], preferred_element_type=jnp.float32)
    return stream.astype(jnp.bfloat16).reshape(grid_h, grid_w, D)
```

```python
import functools

import jax
import jax.numpy as jnp
from jax import lax
from jax.experimental import pallas as pl
from jax.experimental.pallas import tpu as pltpu
from jax.sharding import PartitionSpec as P

HEADS = 16
RADIUS = 4
TOK_H = 32
PATCH = 8
BAND = 8

VMEM = pl.BlockSpec(memory_space=pltpu.VMEM)
SMEM = pl.BlockSpec(memory_space=pltpu.SMEM)


def place_kernel(capacity, empty, dest, offsets, profile, scans, payload, meta, count):
    blocks = scans.shape[0]
    slots = payload.shape[0]
    payload[...] = jnp.zeros_like(payload)

    def clear_slot(i, c):
        meta[i] = empty
        return c

    def clear_count(i, c):
        count[i] = 0
        return c

    lax.fori_loop(0, slots, clear_slot, 0, unroll=8)
    lax.fori_loop(0, slots // capacity, clear_count, 0, unroll=8)

    def put(b, c):
        tile = dest[b]
        rank = count[tile]
        count[tile] = rank + 1
        slot = tile * capacity + rank
        meta[slot] = profile[b] * 256 + offsets[b]
        payload[slot] = scans[b].astype(jnp.bfloat16)
        return c

    lax.fori_loop(0, blocks, put, 0, unroll=4)


def normed(stream, gain_row):
    centre = jnp.mean(stream, -1, keepdims=True)
    spread = jnp.mean(jnp.square(stream - centre), -1, keepdims=True)
    return ((stream - centre) * lax.rsqrt(spread + 1e-05) * gain_row).astype(jnp.bfloat16)


def merge_kernel(meta, got, weights, embed, gain, stream, inputs, num, den, turned):
    slots = got.shape[0]
    rows = got.shape[1]
    lanes = got.shape[2]
    num[...] = jnp.zeros_like(num)
    den[...] = jnp.ones_like(den)

    def add(s, c):
        m = meta[s]
        w = weights[m // 256]
        at = pl.ds(pl.multiple_of((m % 256) * 8, 8), rows)
        num[at, :] += got[s].astype(jnp.float32) * w
        den[at, :] += w
        return c

    lax.fori_loop(0, slots, add, 0, unroll=4)
    group = PATCH * 8

    def turn(i, c):
        at = pl.ds(pl.multiple_of(i * group, group), group)
        merged = (num[at, :] / den[at, :]).astype(jnp.bfloat16).astype(jnp.float32)
        turned[pl.ds(pl.multiple_of(i * lanes, lanes), lanes), :] = merged.T
        return c

    lax.fori_loop(0, TOK_H, turn, 0, unroll=4)
    part = 128

    def embed_part(k, c):
        total = None
        for q in range(PATCH):
            lhs = turned[pl.ds(k * part * PATCH + q, part, stride=PATCH), :]
            term = jnp.dot(
                lhs.astype(jnp.bfloat16), embed[q], preferred_element_type=jnp.float32
            )
            total = term if total is None else total + term
        at = pl.ds(pl.multiple_of(k * part, part), part)
        stream[at, :] = total
        inputs[at, :] = normed(total, gain[...])
        return c

    lax.fori_loop(0, stream.shape[0] // part, embed_part, 0)


def layer_kernel(
    last, token_cols, centre, side, qkv, out_w, stream, bias, gain, *refs
):
    if last:
        tokens, q_ref, kc, ks = refs
    else:
        new_stream, inputs, q_ref, kc, ks = refs
    width = out_w.shape[0]
    head_dim = width // HEADS
    count = stream.shape[0]
    top = RADIUS * token_cols
    step = 512

    def project(n, c):
        cols = pl.ds(pl.multiple_of(n * step, step), step)
        q_ref[:, cols] = (
            jnp.dot(
                centre[top : top + count, :], qkv[:, cols], preferred_element_type=jnp.float32
            ).astype(jnp.bfloat16)
            * head_dim ** (-0.5)
        ).astype(jnp.bfloat16)
        return c

    def project_kv(n, c):
        cols = pl.ds(pl.multiple_of(n * step, step), step)
        from_cols = pl.ds(pl.multiple_of(width + n * step, step), step)
        w = qkv[:, from_cols]
        kc[:, cols] = jnp.dot(centre[...], w, preferred_element_type=jnp.float32).astype(
            jnp.bfloat16
        )
        ks[:, cols] = jnp.dot(side[...], w, preferred_element_type=jnp.float32).astype(
            jnp.bfloat16
        )
        return c

    lax.fori_loop(0, width // step, project, 0)
    lax.fori_loop(0, 2 * width // step, project_kv, 0)
    queries = BAND * token_cols
    c_keys = (BAND + 2 * RADIUS) * token_cols
    s_keys = (BAND + 2 * RADIUS) * 2 * RADIUS
    pair = 2 * head_dim
    low = lax.broadcasted_iota(jnp.int32, (queries, pair), 1) < head_dim

    def band(b, carry):
        q_at = pl.ds(pl.multiple_of(b * queries, queries), queries)
        c_at = pl.ds(pl.multiple_of(b * queries, queries), c_keys)
        s_at = pl.ds(pl.multiple_of(b * BAND * 2 * RADIUS, BAND * 2 * RADIUS), s_keys)
        band_bias = bias[b]
        both = jnp.concatenate([band_bias, band_bias], 0)
        ones = jnp.ones((c_keys + s_keys, pair), jnp.bfloat16)
        pieces = []
        for h in range(HEADS // 2):
            cols = slice(h * pair, (h + 1) * pair)
            v_cols = slice(width + h * pair, width + (h + 1) * pair)
            q = q_ref[q_at, cols]
            zero = jnp.zeros_like(q)
            q2 = jnp.concatenate([jnp.where(low, q, zero), jnp.where(low, zero, q)], 0)
            k = jnp.concatenate([kc[c_at, cols], ks[s_at, cols]], 0)
            v = jnp.concatenate([kc[c_at, v_cols], ks[s_at, v_cols]], 0)
            logits = lax.dot_general(
                q2, k, (((1,), (1,)), ((), ())), preferred_element_type=jnp.float32
            )
            logits = logits + both
            top_logit = jnp.max(logits, -1, keepdims=True)
            weight = jnp.exp(logits - top_logit).astype(jnp.bfloat16)
            summed = jnp.dot(
                weight, jnp.concatenate([v, ones], 1), preferred_element_type=jnp.float32
            )
            share = summed[:, :pair] / summed[:, pair:]
            pieces.append(jnp.where(low, share[:queries], share[queries:]).astype(jnp.bfloat16))
        attended = jnp.concatenate(pieces, 1)
        total = stream[q_at, :] + jnp.dot(
            attended, out_w[...], preferred_element_type=jnp.float32
        )
        if last:
            tokens[q_at, :] = total.astype(jnp.bfloat16)
        else:
            new_stream[q_at, :] = total
            inputs[q_at, :] = normed(total, gain[...])
        return carry

    lax.fori_loop(0, count // queries, band, 0)


def shifted(cells, axis, up):
    count = lax.axis_size(axis)
    pairs = [(i, i + 1) if up else (i + 1, i) for i in range(count - 1)]
    return lax.ppermute(cells, axis, pairs)


def surround(inputs, token_cols):
    width = inputs.shape[-1]
    cells = inputs.reshape(TOK_H, token_cols, width)
    centre = jnp.concatenate(
        [
            shifted(cells[TOK_H - RADIUS :], "row", True),
            cells,
            shifted(cells[:RADIUS], "row", False),
        ],
        0,
    )
    side = jnp.concatenate(
        [
            shifted(centre[:, token_cols - RADIUS :], "col", True),
            shifted(centre[:, :RADIUS], "col", False),
        ],
        1,
    )
    return centre.reshape(-1, width), side.reshape(-1, width)


def window_bias(token_cols):
    bands = TOK_H // BAND
    win = BAND + 2 * RADIUS
    q = jnp.arange(BAND * token_cols, dtype=jnp.int32)
    q_row, q_col = q // token_cols, q % token_cols
    c = jnp.arange(win * token_cols, dtype=jnp.int32)
    s = jnp.arange(win * 2 * RADIUS, dtype=jnp.int32)
    s_off = s % (2 * RADIUS)
    k_row = jnp.concatenate([c // token_cols, s // (2 * RADIUS)]) - RADIUS
    k_col = jnp.concatenate(
        [c % token_cols, jnp.where(s_off < RADIUS, s_off - RADIUS, token_cols + s_off - RADIUS)]
    )
    near = (jnp.abs(k_row[None] - q_row[:, None]) <= RADIUS) & (
        jnp.abs(k_col[None] - q_col[:, None]) <= RADIUS
    )
    g_row = (
        lax.axis_index("row") * TOK_H
        + jnp.arange(bands, dtype=jnp.int32)[:, None] * BAND
        + k_row[None]
    )
    g_col = lax.axis_index("col") * token_cols + k_col
    inside = (
        (g_row >= 0)
        & (g_row < TOK_H * lax.axis_size("row"))
        & (g_col >= 0)[None]
        & (g_col < token_cols * lax.axis_size("col"))[None]
    )
    return jnp.where(near[None] & inside[:, None, :], 0.0, -1e30).astype(jnp.float32)


def per_device(
    scans, dest, offsets, profile_index, profiles, embed_weight, attn_gain, qkv_weight, out_weight
):
    device_count = lax.axis_size("row") * lax.axis_size("col")
    blocks, strip_rows, channels, tile_cols = scans.shape
    token_cols = tile_cols // PATCH
    count = TOK_H * token_cols
    tile_rows = TOK_H * PATCH
    profile_count = profiles.shape[0]
    width = embed_weight.shape[1]
    layers = qkv_weight.shape[0]
    capacity = max(2, 2 * blocks // device_count)
    slots = device_count * capacity
    rows = strip_rows * channels
    f32, bf16 = jnp.float32, jnp.bfloat16
    params = pltpu.CompilerParams(vmem_limit_bytes=56 * 2**20)

    payload, meta = pl.pallas_call(
        functools.partial(place_kernel, capacity, profile_count * 256),
        out_shape=(
            jax.ShapeDtypeStruct((slots, rows, tile_cols), bf16),
            jax.ShapeDtypeStruct((slots,), jnp.int32),
        ),
        in_specs=[SMEM, SMEM, SMEM, VMEM],
        out_specs=(VMEM, SMEM),
        scratch_shapes=[pltpu.SMEM((device_count,), jnp.int32)],
        compiler_params=params,
        name="place",
    )(dest[:, 0], offsets, profile_index, scans.reshape(blocks, rows, tile_cols))
    exchange = functools.partial(
        lax.all_to_all, axis_name=("row", "col"), split_axis=0, concat_axis=0, tiled=True
    )
    got_meta = exchange(meta.reshape(device_count, capacity)).reshape(slots)
    got = exchange(payload.reshape(device_count, capacity * rows, tile_cols))
    got = got.reshape(slots, rows, tile_cols)
    weights = jnp.broadcast_to(
        profiles[:, :, None, :], (profile_count, strip_rows, channels, tile_cols)
    ).reshape(profile_count, rows, tile_cols)
    weights = jnp.concatenate([weights, jnp.zeros((1, rows, tile_cols), f32)], 0)
    embed = (
        embed_weight.reshape(channels, PATCH, PATCH, width)
        .transpose(2, 1, 0, 3)
        .reshape(PATCH, PATCH * channels, width)
    )
    bias = window_bias(token_cols)
    stream, inputs = pl.pallas_call(
        merge_kernel,
        out_shape=(
            jax.ShapeDtypeStruct((count, width), f32),
            jax.ShapeDtypeStruct((count, width), bf16),
        ),
        in_specs=[SMEM, VMEM, VMEM, VMEM, VMEM],
        out_specs=(VMEM, VMEM),
        scratch_shapes=[
            pltpu.VMEM((tile_rows * channels, tile_cols), f32),
            pltpu.VMEM((tile_rows * channels, tile_cols), f32),
            pltpu.VMEM((TOK_H * tile_cols, PATCH * channels), f32),
        ],
        compiler_params=params,
        name="merge",
    )(got_meta, got, weights, embed, attn_gain[:1])
    padded = (TOK_H + 2 * RADIUS) * token_cols
    beside = (TOK_H + 2 * RADIUS) * 2 * RADIUS
    for l in range(layers):
        last = l == layers - 1
        centre, side = surround(inputs, token_cols)
        if last:
            shapes = jax.ShapeDtypeStruct((count, width), bf16)
            specs = VMEM
        else:
            shapes = (
                jax.ShapeDtypeStruct((count, width), f32),
                jax.ShapeDtypeStruct((count, width), bf16),
            )
            specs = (VMEM, VMEM)
        result = pl.pallas_call(
            functools.partial(layer_kernel, last, token_cols),
            out_shape=shapes,
            grid=(1,),
            in_specs=[
                VMEM,
                VMEM,
                pl.BlockSpec((None, width, 3 * width), lambda i, l=l: (l, 0, 0)),
                pl.BlockSpec((None, width, width), lambda i, l=l: (l, 0, 0)),
                VMEM,
                VMEM,
                VMEM,
            ],
            out_specs=specs,
            scratch_shapes=[
                pltpu.VMEM((count, width), bf16),
                pltpu.VMEM((padded, 2 * width), bf16),
                pltpu.VMEM((beside, 2 * width), bf16),
            ],
            compiler_params=params,
            name="layer",
        )(centre, side, qkv_weight, out_weight, stream, bias, attn_gain[min(l + 1, layers - 1)][None])
        if last:
            return result.reshape(TOK_H, token_cols, width)
        stream, inputs = result


def solution(mesh):
    placed = (
        P(("row", "col"), None, None, None),
        P(("row", "col"), None),
        P(("row", "col")),
        P(("row", "col")),
        P(),
        P(),
        P(),
        P(),
        P(),
    )
    return jax.shard_map(
        per_device, mesh=mesh, in_specs=placed, out_specs=P("row", "col", None), check_vma=False
    )
```

```python
import functools

import jax
import jax.numpy as jnp
from jax import lax
from jax.experimental import pallas as pl
from jax.experimental.pallas import tpu as pltpu
from jax.sharding import PartitionSpec as P

HEADS = 16
RADIUS = 4
TOK_H = 32
PATCH = 8
BAND = 8

VMEM = pl.BlockSpec(memory_space=pltpu.VMEM)
SMEM = pl.BlockSpec(memory_space=pltpu.SMEM)


def place_kernel(capacity, dest, offsets, profile, scans, payload, index, count):
    blocks, rows, lanes = scans.shape
    tiles = payload.shape[0]
    payload[...] = jnp.zeros_like(payload)
    index[...] = jnp.zeros_like(index)
    first = lax.broadcasted_iota(jnp.int32, (1, lanes), 1) < lanes // 2

    def clear(i, c):
        count[i] = 0
        return c

    lax.fori_loop(0, tiles, clear, 0, unroll=8)

    def put(b, c):
        tile = dest[b]
        rank = count[tile]
        count[tile] = rank + 1
        payload[tile, pl.ds(pl.multiple_of(rank * rows, rows), rows), :] = scans[b].astype(
            jnp.bfloat16
        )
        named = jnp.where(first, offsets[b], profile[b] + 1).astype(jnp.float32)
        index[tile, pl.ds(rank, 1), :] = named
        return c

    lax.fori_loop(0, blocks, put, 0, unroll=4)
    payload[:, capacity * rows :, :] = index[...].astype(jnp.bfloat16)


def normed(stream, gain_row):
    centre = jnp.mean(stream, -1, keepdims=True)
    spread = jnp.mean(jnp.square(stream - centre), -1, keepdims=True)
    return ((stream - centre) * lax.rsqrt(spread + 1e-05) * gain_row).astype(jnp.bfloat16)


def edges(cells, token_cols):
    tokens = cells.shape[0]
    each = tokens // token_cols * RADIUS
    slot = lax.broadcasted_iota(jnp.int32, (2 * each, tokens), 0)
    token = lax.broadcasted_iota(jnp.int32, (2 * each, tokens), 1)
    right = slot >= each
    slot = jnp.where(right, slot - each, slot)
    col = slot % RADIUS + jnp.where(right, token_cols - RADIUS, 0)
    chosen = (token == slot // RADIUS * token_cols + col).astype(jnp.float32)
    picked = jnp.dot(
        chosen.astype(jnp.bfloat16), cells, preferred_element_type=jnp.float32
    ).astype(jnp.bfloat16)
    return picked[:each], picked[each:]


def merge_kernel(
    rows, token_cols, meta, got, weights, embed, gain, stream, inputs, left, right, num, den, turned
):
    tiles, _, lanes = got.shape
    capacity = meta.shape[0] // tiles
    num[...] = jnp.zeros_like(num)
    den[...] = jnp.ones_like(den)

    def add_tile(t, c):
        for r in range(capacity):
            m = meta[t * capacity + r]
            w = weights[m >> 8]
            at = pl.ds(pl.multiple_of((m & 255) * 8, 8), rows)
            num[at, :] += got[t, r * rows : (r + 1) * rows, :].astype(jnp.float32) * w
            den[at, :] += w
        return c

    lax.fori_loop(0, tiles, add_tile, 0)
    group = PATCH * 8

    def turn(i, c):
        at = pl.ds(pl.multiple_of(i * group, group), group)
        merged = (num[at, :] / den[at, :]).astype(jnp.bfloat16).astype(jnp.float32)
        turned[pl.ds(pl.multiple_of(i * lanes, lanes), lanes), :] = merged.T
        return c

    lax.fori_loop(0, TOK_H, turn, 0, unroll=4)
    part = BAND * token_cols

    def embed_part(k, c):
        total = None
        for q in range(PATCH):
            lhs = turned[pl.ds(k * part * PATCH + q, part, stride=PATCH), :]
            term = jnp.dot(
                lhs.astype(jnp.bfloat16), embed[q], preferred_element_type=jnp.float32
            )
            total = term if total is None else total + term
        at = pl.ds(pl.multiple_of(k * part, part), part)
        stream[at, :] = total
        cells = normed(total, gain[...])
        inputs[at, :] = cells
        edge = pl.ds(pl.multiple_of(k * BAND * RADIUS, BAND * RADIUS), BAND * RADIUS)
        left[edge, :], right[edge, :] = edges(cells, token_cols)
        return c

    lax.fori_loop(0, TOK_H // BAND, embed_part, 0)


def layer_kernel(layer, last, token_cols, sizes, x, own_left, own_right, qkv, out_w, stream, bias, gain, *refs):
    outs, refs = (refs[:1], refs[1:]) if last else (refs[:4], refs[4:])
    q_ref, kc, kl, kr, w, wo, x_rows, x_left, x_right, w_sem, send, recv = refs
    width = wo.shape[0]
    head_dim = width // HEADS
    count = x.shape[0]
    halo = RADIUS * token_cols
    corner = RADIUS * RADIUS
    side = TOK_H * RADIUS
    loads = [
        pltpu.make_async_copy(
            qkv.at[layer, :, n * width : (n + 1) * width], w.at[n], w_sem.at[n]
        )
        for n in range(3)
    ] + [pltpu.make_async_copy(out_w.at[layer], wo, w_sem.at[3])]
    for load in loads:
        load.start()

    row, col = lax.axis_index("row"), lax.axis_index("col")
    up, down = row > 0, row < sizes[0] - 1
    west, east = col > 0, col < sizes[1] - 1
    moves = [
        (-1, 0, up, x.at[:halo], x_rows.at[halo:], x_rows.at[:halo]),
        (1, 0, down, x.at[count - halo :], x_rows.at[:halo], x_rows.at[halo:]),
        (0, -1, west, own_left, x_right.at[corner : corner + side], x_left.at[corner : corner + side]),
        (0, 1, east, own_right, x_left.at[corner : corner + side], x_right.at[corner : corner + side]),
        (-1, -1, up & west, own_left.at[:corner], x_right.at[corner + side :], x_left.at[:corner]),
        (-1, 1, up & east, own_right.at[:corner], x_left.at[corner + side :], x_right.at[:corner]),
        (1, -1, down & west, own_left.at[side - corner :], x_right.at[:corner], x_left.at[corner + side :]),
        (1, 1, down & east, own_right.at[side - corner :], x_left.at[:corner], x_right.at[corner + side :]),
    ]
    opposite = [1, 0, 3, 2, 7, 6, 5, 4]
    barrier = pltpu.get_barrier_semaphore()
    mesh_ids = pl.DeviceIdType.MESH
    for dr, dc, there, _, _, _ in moves:

        @pl.when(there)
        def _(dr=dr, dc=dc):
            pl.semaphore_signal(
                barrier, inc=1, device_id=(row + dr, col + dc), device_id_type=mesh_ids
            )

    for _, _, there, _, _, here in moves:

        @pl.when(jnp.logical_not(there))
        def _(here=here):
            here[...] = jnp.zeros(here.shape, here.dtype)

    rows_near = 1 + up.astype(jnp.int32) + down.astype(jnp.int32)
    cols_near = 1 + west.astype(jnp.int32) + east.astype(jnp.int32)
    pl.semaphore_wait(barrier, rows_near * cols_near - 1)
    copies = []
    for n, (dr, dc, there, source, lands, _) in enumerate(moves):
        copies.append(
            pltpu.make_async_remote_copy(
                src_ref=source,
                dst_ref=lands,
                send_sem=send.at[n],
                recv_sem=recv.at[n],
                device_id=(row + dr, col + dc),
                device_id_type=mesh_ids,
            )
        )

        @pl.when(there)
        def _(copy=copies[-1]):
            copy.start()

    def times(rows, weight, target, at, base, scale=None):
        step = 512

        def part(n, c):
            cols = pl.ds(pl.multiple_of(n * step, step), step)
            to = pl.ds(pl.multiple_of(base + n * step, step), step)
            y = jnp.dot(
                rows[...], weight[:, cols], preferred_element_type=jnp.float32
            ).astype(jnp.bfloat16)
            target[at, to] = y if scale is None else (y * scale).astype(jnp.bfloat16)
            return c

        lax.fori_loop(0, width // step, part, 0)

    middle = slice(halo, halo + count)
    loads[0].wait()
    times(x, w.at[0], q_ref, slice(0, count), 0, head_dim ** (-0.5))
    for n in (1, 2):
        loads[n].wait()
        times(x, w.at[n], kc, middle, (n - 1) * width)
    for n, (_, _, there, _, _, here) in enumerate(moves):

        @pl.when(there)
        def _(n=n, here=here):
            copies[n].wait_send()
            pltpu.make_async_remote_copy(
                src_ref=here,
                dst_ref=here,
                send_sem=send.at[n],
                recv_sem=recv.at[opposite[n]],
                device_id=(row + moves[n][0], col + moves[n][1]),
                device_id_type=mesh_ids,
            ).wait_recv()

    for n in (1, 2):
        base = (n - 1) * width
        times(x_rows.at[:halo], w.at[n], kc, slice(0, halo), base)
        times(x_rows.at[halo:], w.at[n], kc, slice(halo + count, 2 * halo + count), base)
        times(x_left, w.at[n], kl, slice(0, side + 2 * corner), base)
        times(x_right, w.at[n], kr, slice(0, side + 2 * corner), base)
    loads[3].wait()
    queries = BAND * token_cols
    c_keys = (BAND + 2 * RADIUS) * token_cols
    s_keys = (BAND + 2 * RADIUS) * RADIUS
    pair = 2 * head_dim
    low = lax.broadcasted_iota(jnp.int32, (queries, pair), 1) < head_dim

    def band(b, carry):
        q_at = pl.ds(pl.multiple_of(b * queries, queries), queries)
        c_at = pl.ds(pl.multiple_of(b * queries, queries), c_keys)
        s_at = pl.ds(pl.multiple_of(b * BAND * RADIUS, BAND * RADIUS), s_keys)
        band_bias = bias[b]
        both = jnp.concatenate([band_bias, band_bias], 0)
        ones = jnp.ones((c_keys + 2 * s_keys, pair), jnp.bfloat16)
        pieces = []
        for h in range(HEADS // 2):
            cols = slice(h * pair, (h + 1) * pair)
            v_cols = slice(width + h * pair, width + (h + 1) * pair)
            q = q_ref[q_at, cols]
            zero = jnp.zeros_like(q)
            q2 = jnp.concatenate([jnp.where(low, q, zero), jnp.where(low, zero, q)], 0)
            k = jnp.concatenate([kc[c_at, cols], kl[s_at, cols], kr[s_at, cols]], 0)
            v = jnp.concatenate([kc[c_at, v_cols], kl[s_at, v_cols], kr[s_at, v_cols]], 0)
            logits = lax.dot_general(
                q2, k, (((1,), (1,)), ((), ())), preferred_element_type=jnp.float32
            )
            logits = logits + both
            top_logit = jnp.max(logits, -1, keepdims=True)
            weight = jnp.exp(logits - top_logit).astype(jnp.bfloat16)
            summed = jnp.dot(
                weight, jnp.concatenate([v, ones], 1), preferred_element_type=jnp.float32
            )
            share = summed[:, :pair] / summed[:, pair:]
            pieces.append(jnp.where(low, share[:queries], share[queries:]).astype(jnp.bfloat16))
        attended = jnp.concatenate(pieces, 1)
        total = stream[q_at, :] + jnp.dot(attended, wo[...], preferred_element_type=jnp.float32)
        if last:
            outs[0][q_at, :] = total.astype(jnp.bfloat16)
        else:
            outs[0][q_at, :] = total
            cells = normed(total, gain[...])
            outs[1][q_at, :] = cells
            edge = pl.ds(pl.multiple_of(b * BAND * RADIUS, BAND * RADIUS), BAND * RADIUS)
            outs[2][edge, :], outs[3][edge, :] = edges(cells, token_cols)
        return carry

    lax.fori_loop(0, count // queries, band, 0)


def window_bias(token_cols):
    bands = TOK_H // BAND
    win = BAND + 2 * RADIUS
    q = jnp.arange(BAND * token_cols, dtype=jnp.int32)
    q_row, q_col = q // token_cols, q % token_cols
    c = jnp.arange(win * token_cols, dtype=jnp.int32)
    s = jnp.arange(win * RADIUS, dtype=jnp.int32)
    k_row = jnp.concatenate([c // token_cols, s // RADIUS, s // RADIUS]) - RADIUS
    k_col = jnp.concatenate([c % token_cols, s % RADIUS - RADIUS, s % RADIUS + token_cols])
    near = (jnp.abs(k_row[None] - q_row[:, None]) <= RADIUS) & (
        jnp.abs(k_col[None] - q_col[:, None]) <= RADIUS
    )
    g_row = (
        lax.axis_index("row") * TOK_H
        + jnp.arange(bands, dtype=jnp.int32)[:, None] * BAND
        + k_row[None]
    )
    g_col = lax.axis_index("col") * token_cols + k_col
    inside = (
        (g_row >= 0)
        & (g_row < TOK_H * lax.axis_size("row"))
        & (g_col >= 0)[None]
        & (g_col < token_cols * lax.axis_size("col"))[None]
    )
    return jnp.where(near[None] & inside[:, None, :], 0.0, -1e30).astype(jnp.float32)


def per_device(
    scans, dest, offsets, profile_index, profiles, embed_weight, attn_gain, qkv_weight, out_weight
):
    device_count = lax.axis_size("row") * lax.axis_size("col")
    blocks, strip_rows, channels, tile_cols = scans.shape
    token_cols = tile_cols // PATCH
    count = TOK_H * token_cols
    tile_rows = TOK_H * PATCH
    profile_count = profiles.shape[0]
    width = embed_weight.shape[1]
    layers = qkv_weight.shape[0]
    capacity = max(2, 2 * blocks // device_count)
    slots = device_count * capacity
    rows = strip_rows * channels
    extra = -(-capacity // 16) * 16
    f32, bf16 = jnp.float32, jnp.bfloat16
    params = pltpu.CompilerParams(vmem_limit_bytes=56 * 2**20)

    payload = pl.pallas_call(
        functools.partial(place_kernel, capacity),
        out_shape=jax.ShapeDtypeStruct((device_count, capacity * rows + extra, tile_cols), bf16),
        in_specs=[SMEM, SMEM, SMEM, VMEM],
        out_specs=VMEM,
        scratch_shapes=[
            pltpu.VMEM((device_count, extra, tile_cols), f32),
            pltpu.SMEM((device_count,), jnp.int32),
        ],
        compiler_params=params,
        name="place",
    )(dest[:, 0], offsets, profile_index, scans.reshape(blocks, rows, tile_cols))
    got = lax.all_to_all(payload, ("row", "col"), split_axis=0, concat_axis=0, tiled=True)
    named = got[:, capacity * rows : capacity * rows + capacity, :]
    meta = (named[:, :, 0] + named[:, :, tile_cols // 2].astype(f32) * 256.0).astype(jnp.int32)
    meta = meta.reshape(slots)
    weights = jnp.broadcast_to(
        profiles[:, :, None, :], (profile_count, strip_rows, channels, tile_cols)
    ).reshape(profile_count, rows, tile_cols)
    weights = jnp.concatenate([jnp.zeros((1, rows, tile_cols), f32), weights], 0)
    embed = (
        embed_weight.reshape(channels, PATCH, PATCH, width)
        .transpose(2, 1, 0, 3)
        .reshape(PATCH, PATCH * channels, width)
    )
    bias = window_bias(token_cols)
    edge = jax.ShapeDtypeStruct((TOK_H * RADIUS, width), bf16)
    state = (
        jax.ShapeDtypeStruct((count, width), f32),
        jax.ShapeDtypeStruct((count, width), bf16),
        edge,
        edge,
    )
    stream, inputs, left, right = pl.pallas_call(
        functools.partial(merge_kernel, rows, token_cols),
        out_shape=state,
        in_specs=[SMEM, VMEM, VMEM, VMEM, VMEM],
        out_specs=(VMEM,) * 4,
        scratch_shapes=[
            pltpu.VMEM((tile_rows * channels, tile_cols), f32),
            pltpu.VMEM((tile_rows * channels, tile_cols), f32),
            pltpu.VMEM((TOK_H * tile_cols, PATCH * channels), f32),
        ],
        compiler_params=params,
        name="merge",
    )(meta, got, weights, embed, attn_gain[:1])
    halo = RADIUS * token_cols
    beside = (TOK_H + 2 * RADIUS) * RADIUS
    sizes = (lax.axis_size("row"), lax.axis_size("col"))
    hbm = pl.BlockSpec(memory_space=pl.ANY)
    for l in range(layers):
        last = l == layers - 1
        result = pl.pallas_call(
            functools.partial(layer_kernel, l, last, token_cols, sizes),
            out_shape=state[1] if last else state,
            in_specs=[VMEM, VMEM, VMEM, hbm, hbm, VMEM, VMEM, VMEM],
            out_specs=VMEM if last else (VMEM,) * 4,
            scratch_shapes=[
                pltpu.VMEM((count, width), bf16),
                pltpu.VMEM((count + 2 * halo, 2 * width), bf16),
                pltpu.VMEM((beside, 2 * width), bf16),
                pltpu.VMEM((beside, 2 * width), bf16),
                pltpu.VMEM((3, width, width), bf16),
                pltpu.VMEM((width, width), bf16),
                pltpu.VMEM((2 * halo, width), bf16),
                pltpu.VMEM((beside, width), bf16),
                pltpu.VMEM((beside, width), bf16),
                pltpu.SemaphoreType.DMA((4,)),
                pltpu.SemaphoreType.DMA((8,)),
                pltpu.SemaphoreType.DMA((8,)),
            ],
            compiler_params=pltpu.CompilerParams(
                vmem_limit_bytes=56 * 2**20, collective_id=l, has_side_effects=True
            ),
            name="layer" + str(l),
        )(
            inputs,
            left,
            right,
            qkv_weight,
            out_weight,
            stream,
            bias,
            attn_gain[min(l + 1, layers - 1)][None],
        )
        if last:
            return result.reshape(TOK_H, token_cols, width)
        stream, inputs, left, right = result


def solution(mesh):
    placed = (
        P(("row", "col"), None, None, None),
        P(("row", "col"), None),
        P(("row", "col")),
        P(("row", "col")),
        P(),
        P(),
        P(),
        P(),
        P(),
    )
    return jax.shard_map(
        per_device, mesh=mesh, in_specs=placed, out_specs=P("row", "col", None), check_vma=False
    )
```

```python
import functools

import jax
import jax.numpy as jnp
from jax import lax
from jax.experimental import pallas as pl
from jax.experimental.pallas import tpu as pltpu
from jax.sharding import PartitionSpec as P

HEADS = 16
RADIUS = 4
TOK_H = 32
PATCH = 8
BAND = 8

VMEM = pl.BlockSpec(memory_space=pltpu.VMEM)
SMEM = pl.BlockSpec(memory_space=pltpu.SMEM)


def place_kernel(capacity, dest, offsets, profile, scans, payload, index, count):
    blocks, rows, lanes = scans.shape
    tiles = payload.shape[0]
    payload[...] = jnp.zeros_like(payload)
    index[...] = jnp.zeros_like(index)
    first = lax.broadcasted_iota(jnp.int32, (1, lanes), 1) < lanes // 2

    def clear(i, c):
        count[i] = 0
        return c

    lax.fori_loop(0, tiles, clear, 0, unroll=8)

    def put(b, c):
        tile = dest[b]
        rank = count[tile]
        count[tile] = rank + 1
        payload[tile, pl.ds(pl.multiple_of(rank * rows, rows), rows), :] = scans[b].astype(
            jnp.bfloat16
        )
        named = jnp.where(first, offsets[b], profile[b] + 1).astype(jnp.float32)
        index[tile, pl.ds(rank, 1), :] = named
        return c

    lax.fori_loop(0, blocks, put, 0, unroll=4)
    payload[:, capacity * rows :, :] = index[...].astype(jnp.bfloat16)


def normed(stream, gain_row):
    centre = jnp.mean(stream, -1, keepdims=True)
    spread = jnp.mean(jnp.square(stream - centre), -1, keepdims=True)
    return ((stream - centre) * lax.rsqrt(spread + 1e-05) * gain_row).astype(jnp.bfloat16)


def regroup(token_cols, back=False):
    tokens = BAND * token_cols
    each = BAND * RADIUS
    shape = (tokens, tokens)
    grouped = lax.broadcasted_iota(jnp.int32, shape, 1 if back else 0)
    natural = lax.broadcasted_iota(jnp.int32, shape, 0 if back else 1)
    inner = grouped % each
    source = inner // RADIUS * token_cols + grouped // each * RADIUS + inner % RADIUS
    return (natural == source).astype(jnp.float32).astype(jnp.bfloat16)


def store_band(b, total, cells, stream, inputs):
    each = BAND * RADIUS
    units = each // inputs.shape[2]
    at = pl.ds(pl.multiple_of(b * each, each), each)
    for g in range(inputs.shape[0]):
        rows = slice(g * each, (g + 1) * each)
        stream[g, at, :] = total[rows]
        inputs[g, pl.ds(b * units, units)] = cells[rows].reshape(
            units, each // units, cells.shape[1]
        )


def merge_kernel(
    rows, token_cols, meta, got, weights, embed, gain, stream, inputs, num, den, turned
):
    tiles, _, lanes = got.shape
    capacity = meta.shape[0] // tiles
    num[...] = jnp.zeros_like(num)
    den[...] = jnp.ones_like(den)

    def add_tile(t, c):
        for r in range(capacity):
            m = meta[t * capacity + r]
            w = weights[m >> 8]
            at = pl.ds(pl.multiple_of((m & 255) * 8, 8), rows)
            num[at, :] += got[t, r * rows : (r + 1) * rows, :].astype(jnp.float32) * w
            den[at, :] += w
        return c

    lax.fori_loop(0, tiles, add_tile, 0)
    group = PATCH * 8

    def turn(i, c):
        at = pl.ds(pl.multiple_of(i * group, group), group)
        merged = (num[at, :] / den[at, :]).astype(jnp.bfloat16).astype(jnp.float32)
        turned[pl.ds(pl.multiple_of(i * lanes, lanes), lanes), :] = merged.T
        return c

    lax.fori_loop(0, TOK_H, turn, 0, unroll=4)
    part = BAND * token_cols
    order = regroup(token_cols)

    def embed_part(k, c):
        total = None
        for q in range(PATCH):
            lhs = turned[pl.ds(k * part * PATCH + q, part, stride=PATCH), :]
            lhs = jnp.dot(order, lhs.astype(jnp.bfloat16), preferred_element_type=jnp.float32)
            term = jnp.dot(
                lhs.astype(jnp.bfloat16), embed[q], preferred_element_type=jnp.float32
            )
            total = term if total is None else total + term
        store_band(k, total, normed(total, gain[...]), stream, inputs)
        return c

    lax.fori_loop(0, TOK_H // BAND, embed_part, 0)


def layer_kernel(layer, last, token_cols, sizes, x, qkv, out_w, stream, bias, gain, *refs):
    outs, refs = (refs[:1], refs[1:]) if last else (refs[:2], refs[2:])
    q_ref, kv, w, wo, xh, w_sem, send, recv = refs
    width = wo.shape[0]
    head_dim = width // HEADS
    groups, units, unit, _ = x.shape
    own = units * unit
    count = groups * own
    loads = [
        pltpu.make_async_copy(
            qkv.at[layer, :, n * width : (n + 1) * width], w.at[n], w_sem.at[n]
        )
        for n in range(3)
    ] + [pltpu.make_async_copy(out_w.at[layer], wo, w_sem.at[3])]
    for load in loads:
        load.start()

    row, col = lax.axis_index("row"), lax.axis_index("col")
    up, down = row > 0, row < sizes[0] - 1
    west, east = col > 0, col < sizes[1] - 1
    top, bottom = xh.at[:groups], xh.at[groups : 2 * groups]
    l0 = 2 * groups
    r0 = l0 + units + 2
    end = r0 + units + 2
    moves = [
        (-1, 0, up, x.at[:, 0], bottom, top),
        (1, 0, down, x.at[:, units - 1], top, bottom),
        (0, -1, west, x.at[0], xh.at[r0 + 1 : end - 1], xh.at[l0 + 1 : r0 - 1]),
        (0, 1, east, x.at[groups - 1], xh.at[l0 + 1 : r0 - 1], xh.at[r0 + 1 : end - 1]),
        (-1, -1, up & west, x.at[0, 0], xh.at[end - 1], xh.at[l0]),
        (-1, 1, up & east, x.at[groups - 1, 0], xh.at[r0 - 1], xh.at[r0]),
        (1, -1, down & west, x.at[0, units - 1], xh.at[r0], xh.at[r0 - 1]),
        (1, 1, down & east, x.at[groups - 1, units - 1], xh.at[l0], xh.at[end - 1]),
    ]
    opposite = [1, 0, 3, 2, 7, 6, 5, 4]
    barrier = pltpu.get_barrier_semaphore()
    mesh_ids = pl.DeviceIdType.MESH
    for dr, dc, there, _, _, _ in moves:

        @pl.when(there)
        def _(dr=dr, dc=dc):
            pl.semaphore_signal(
                barrier, inc=1, device_id=(row + dr, col + dc), device_id_type=mesh_ids
            )

    for _, _, there, _, _, here in moves:

        @pl.when(jnp.logical_not(there))
        def _(here=here):
            here[...] = jnp.zeros(here.shape, here.dtype)

    rows_near = 1 + up.astype(jnp.int32) + down.astype(jnp.int32)
    cols_near = 1 + west.astype(jnp.int32) + east.astype(jnp.int32)
    pl.semaphore_wait(barrier, rows_near * cols_near - 1)
    copies = []
    for n, (dr, dc, there, source, lands, _) in enumerate(moves):
        copies.append(
            pltpu.make_async_remote_copy(
                src_ref=source,
                dst_ref=lands,
                send_sem=send.at[n],
                recv_sem=recv.at[n],
                device_id=(row + dr, col + dc),
                device_id_type=mesh_ids,
            )
        )

        @pl.when(there)
        def _(copy=copies[-1]):
            copy.start()

    step = 512

    def project(n, put):
        rows = x if n < 3 else xh
        weight = w.at[n] if n < 3 else w.at[n - 2]
        total = count if n < 3 else end * unit

        def part(k, c):
            cols = pl.ds(pl.multiple_of(k * step, step), step)
            y = jnp.dot(
                rows[...].reshape(total, width),
                weight[:, cols],
                preferred_element_type=jnp.float32,
            ).astype(jnp.bfloat16)
            put(k, y)
            return c

        lax.fori_loop(0, width // step, part, 0)

    def put_q(k, y):
        cols = pl.ds(pl.multiple_of(k * step, step), step)
        for g in range(groups):
            q_ref[g, :, cols] = (y[g * own : (g + 1) * own] * head_dim ** (-0.5)).astype(
                jnp.bfloat16
            )

    def put_own(base, k, y):
        cols = pl.ds(pl.multiple_of(base + k * step, step), step)
        for g in range(groups):
            kv[g + 1, unit : unit + own, cols] = y[g * own : (g + 1) * own]

    def put_halo(base, k, y):
        cols = pl.ds(pl.multiple_of(base + k * step, step), step)
        for g in range(groups):
            kv[g + 1, :unit, cols] = y[g * unit : (g + 1) * unit]
            kv[g + 1, unit + own :, cols] = y[(groups + g) * unit : (groups + g + 1) * unit]
        kv[0, :, cols] = y[l0 * unit : r0 * unit]
        kv[groups + 1, :, cols] = y[r0 * unit :]

    loads[0].wait()
    project(0, put_q)
    for n in (1, 2):
        loads[n].wait()
        project(n, functools.partial(put_own, (n - 1) * width))
    for n, (_, _, there, _, _, here) in enumerate(moves):

        @pl.when(there)
        def _(n=n, here=here):
            copies[n].wait_send()
            pltpu.make_async_remote_copy(
                src_ref=here,
                dst_ref=here,
                send_sem=send.at[n],
                recv_sem=recv.at[opposite[n]],
                device_id=(row + moves[n][0], col + moves[n][1]),
                device_id_type=mesh_ids,
            ).wait_recv()

    for n in (3, 4):
        project(n, functools.partial(put_halo, (n - 3) * width))
    loads[3].wait()
    each = BAND * RADIUS
    span = (BAND + 2 * RADIUS) * RADIUS
    pair = 2 * head_dim
    queries = 2 * each
    low = lax.broadcasted_iota(jnp.int32, (queries, pair), 1) < head_dim
    ones = jnp.ones((4 * span, pair), jnp.bfloat16)
    order = regroup(token_cols, True) if last else None

    def band(b, carry):
        q_at = pl.ds(pl.multiple_of(b * each, each), each)
        k_at = pl.ds(pl.multiple_of(b * each, each), span)
        halves = []
        for s in range(groups // 2):
            half_bias = bias[b, s]
            both = jnp.concatenate([half_bias, half_bias], 0)
            pieces = []
            for h in range(HEADS // 2):
                cols = slice(h * pair, (h + 1) * pair)
                v_cols = slice(width + h * pair, width + (h + 1) * pair)
                q = jnp.concatenate([q_ref[2 * s + i, q_at, cols] for i in range(2)], 0)
                zero = jnp.zeros_like(q)
                q2 = jnp.concatenate([jnp.where(low, q, zero), jnp.where(low, zero, q)], 0)
                k = jnp.concatenate([kv[2 * s + i, k_at, cols] for i in range(4)], 0)
                v = jnp.concatenate([kv[2 * s + i, k_at, v_cols] for i in range(4)], 0)
                logits = lax.dot_general(
                    q2, k, (((1,), (1,)), ((), ())), preferred_element_type=jnp.float32
                )
                logits = logits + both
                top_logit = jnp.max(logits, -1, keepdims=True)
                weight = jnp.exp(logits - top_logit).astype(jnp.bfloat16)
                summed = jnp.dot(
                    weight, jnp.concatenate([v, ones], 1), preferred_element_type=jnp.float32
                )
                share = summed[:, :pair] / summed[:, pair:]
                pieces.append(
                    jnp.where(low, share[:queries], share[queries:]).astype(jnp.bfloat16)
                )
            halves.append(jnp.concatenate(pieces, 1))
        attended = jnp.concatenate(halves, 0)
        before = jnp.concatenate([stream[g, q_at, :] for g in range(groups)], 0)
        total = before + jnp.dot(attended, wo[...], preferred_element_type=jnp.float32)
        if last:
            rows = BAND * token_cols
            outs[0][pl.ds(pl.multiple_of(b * rows, rows), rows), :] = jnp.dot(
                order, total.astype(jnp.bfloat16), preferred_element_type=jnp.float32
            ).astype(jnp.bfloat16)
        else:
            store_band(b, total, normed(total, gain[...]), outs[0], outs[1])
        return carry

    lax.fori_loop(0, TOK_H // BAND, band, 0)


def window_bias(token_cols):
    bands, halves = TOK_H // BAND, token_cols // (2 * RADIUS)
    win = BAND + 2 * RADIUS
    q = jnp.arange(2 * BAND * RADIUS, dtype=jnp.int32)
    k = jnp.arange(4 * win * RADIUS, dtype=jnp.int32)
    q_row = q % (BAND * RADIUS) // RADIUS
    q_col = q // (BAND * RADIUS) * RADIUS + q % RADIUS
    k_row = k % (win * RADIUS) // RADIUS - RADIUS
    k_col = k // (win * RADIUS) * RADIUS + k % RADIUS - RADIUS
    near = (jnp.abs(k_row[None] - q_row[:, None]) <= RADIUS) & (
        jnp.abs(k_col[None] - q_col[:, None]) <= RADIUS
    )
    g_row = (
        lax.axis_index("row") * TOK_H
        + jnp.arange(bands, dtype=jnp.int32)[:, None] * BAND
        + k_row[None]
    )
    g_col = (
        lax.axis_index("col") * token_cols
        + jnp.arange(halves, dtype=jnp.int32)[:, None] * 2 * RADIUS
        + k_col[None]
    )
    row_in = (g_row >= 0) & (g_row < TOK_H * lax.axis_size("row"))
    col_in = (g_col >= 0) & (g_col < token_cols * lax.axis_size("col"))
    inside = row_in[:, None] & col_in[None]
    return jnp.where(near[None, None] & inside[:, :, None], 0.0, -1e30).astype(jnp.float32)


def per_device(
    scans, dest, offsets, profile_index, profiles, embed_weight, attn_gain, qkv_weight, out_weight
):
    device_count = lax.axis_size("row") * lax.axis_size("col")
    blocks, strip_rows, channels, tile_cols = scans.shape
    token_cols = tile_cols // PATCH
    count = TOK_H * token_cols
    tile_rows = TOK_H * PATCH
    profile_count = profiles.shape[0]
    width = embed_weight.shape[1]
    layers = qkv_weight.shape[0]
    capacity = max(2, 2 * blocks // device_count)
    slots = device_count * capacity
    rows = strip_rows * channels
    extra = -(-capacity // 16) * 16
    f32, bf16 = jnp.float32, jnp.bfloat16
    params = pltpu.CompilerParams(vmem_limit_bytes=56 * 2**20)

    payload = pl.pallas_call(
        functools.partial(place_kernel, capacity),
        out_shape=jax.ShapeDtypeStruct((device_count, capacity * rows + extra, tile_cols), bf16),
        in_specs=[SMEM, SMEM, SMEM, VMEM],
        out_specs=VMEM,
        scratch_shapes=[
            pltpu.VMEM((device_count, extra, tile_cols), f32),
            pltpu.SMEM((device_count,), jnp.int32),
        ],
        compiler_params=params,
        name="place",
    )(dest[:, 0], offsets, profile_index, scans.reshape(blocks, rows, tile_cols))
    got = lax.all_to_all(payload, ("row", "col"), split_axis=0, concat_axis=0, tiled=True)
    named = got[:, capacity * rows : capacity * rows + capacity, :]
    meta = (named[:, :, 0] + named[:, :, tile_cols // 2].astype(f32) * 256.0).astype(jnp.int32)
    meta = meta.reshape(slots)
    weights = jnp.broadcast_to(
        profiles[:, :, None, :], (profile_count, strip_rows, channels, tile_cols)
    ).reshape(profile_count, rows, tile_cols)
    weights = jnp.concatenate([jnp.zeros((1, rows, tile_cols), f32), weights], 0)
    embed = (
        embed_weight.reshape(channels, PATCH, PATCH, width)
        .transpose(2, 1, 0, 3)
        .reshape(PATCH, PATCH * channels, width)
    )
    bias = window_bias(token_cols)
    groups = token_cols // RADIUS
    unit = RADIUS * RADIUS
    units = TOK_H // RADIUS
    state = (
        jax.ShapeDtypeStruct((groups, units * unit, width), f32),
        jax.ShapeDtypeStruct((groups, units, unit, width), bf16),
    )
    stream, inputs = pl.pallas_call(
        functools.partial(merge_kernel, rows, token_cols),
        out_shape=state,
        in_specs=[SMEM, VMEM, VMEM, VMEM, VMEM],
        out_specs=(VMEM,) * 2,
        scratch_shapes=[
            pltpu.VMEM((tile_rows * channels, tile_cols), f32),
            pltpu.VMEM((tile_rows * channels, tile_cols), f32),
            pltpu.VMEM((TOK_H * tile_cols, PATCH * channels), f32),
        ],
        compiler_params=params,
        name="merge",
    )(meta, got, weights, embed, attn_gain[:1])
    sizes = (lax.axis_size("row"), lax.axis_size("col"))
    hbm = pl.BlockSpec(memory_space=pl.ANY)
    for l in range(layers):
        last = l == layers - 1
        result = pl.pallas_call(
            functools.partial(layer_kernel, l, last, token_cols, sizes),
            out_shape=jax.ShapeDtypeStruct((count, width), bf16) if last else state,
            in_specs=[VMEM, hbm, hbm, VMEM, VMEM, VMEM],
            out_specs=VMEM if last else (VMEM,) * 2,
            scratch_shapes=[
                pltpu.VMEM((groups, units * unit, width), bf16),
                pltpu.VMEM((groups + 2, (units + 2) * unit, 2 * width), bf16),
                pltpu.VMEM((3, width, width), bf16),
                pltpu.VMEM((width, width), bf16),
                pltpu.VMEM((2 * groups + 2 * (units + 2), unit, width), bf16),
                pltpu.SemaphoreType.DMA((4,)),
                pltpu.SemaphoreType.DMA((8,)),
                pltpu.SemaphoreType.DMA((8,)),
            ],
            compiler_params=pltpu.CompilerParams(
                vmem_limit_bytes=56 * 2**20, collective_id=l, has_side_effects=True
            ),
            name="layer" + str(l),
        )(
            inputs,
            qkv_weight,
            out_weight,
            stream,
            bias,
            attn_gain[min(l + 1, layers - 1)][None],
        )
        if last:
            return result.reshape(TOK_H, token_cols, width)
        stream, inputs = result


def solution(mesh):
    placed = (
        P(("row", "col"), None, None, None),
        P(("row", "col"), None),
        P(("row", "col")),
        P(("row", "col")),
        P(),
        P(),
        P(),
        P(),
        P(),
    )
    return jax.shard_map(
        per_device, mesh=mesh, in_specs=placed, out_specs=P("row", "col", None), check_vma=False
    )
```

```python
import functools

import jax
import jax.numpy as jnp
from jax import lax
from jax.experimental import pallas as pl
from jax.experimental.pallas import tpu as pltpu
from jax.sharding import PartitionSpec as P

HEADS = 16
RADIUS = 4
TOK_H = 32
PATCH = 8
BAND = 8

VMEM = pl.BlockSpec(memory_space=pltpu.VMEM)
SMEM = pl.BlockSpec(memory_space=pltpu.SMEM)


def place_kernel(capacity, dest, offsets, profile, scans, payload, index, count):
    blocks, rows, lanes = scans.shape
    tiles = payload.shape[0]
    payload[...] = jnp.zeros_like(payload)
    index[...] = jnp.zeros_like(index)
    first = lax.broadcasted_iota(jnp.int32, (1, lanes), 1) < lanes // 2

    def clear(i, c):
        count[i] = 0
        return c

    lax.fori_loop(0, tiles, clear, 0, unroll=8)

    def put(b, c):
        tile = dest[b]
        rank = count[tile]
        count[tile] = rank + 1
        payload[tile, pl.ds(pl.multiple_of(rank * rows, rows), rows), :] = scans[b].astype(
            jnp.bfloat16
        )
        named = jnp.where(first, offsets[b], profile[b] + 1).astype(jnp.float32)
        index[tile, pl.ds(rank, 1), :] = named
        return c

    lax.fori_loop(0, blocks, put, 0, unroll=4)
    payload[:, capacity * rows :, :] = index[...].astype(jnp.bfloat16)


def normed(stream, gain_row):
    centre = jnp.mean(stream, -1, keepdims=True)
    spread = jnp.mean(jnp.square(stream - centre), -1, keepdims=True)
    return ((stream - centre) * lax.rsqrt(spread + 1e-05) * gain_row).astype(jnp.bfloat16)


def regroup(token_cols, back=False):
    tokens = BAND * token_cols
    each = BAND * RADIUS
    shape = (tokens, tokens)
    grouped = lax.broadcasted_iota(jnp.int32, shape, 1 if back else 0)
    natural = lax.broadcasted_iota(jnp.int32, shape, 0 if back else 1)
    inner = grouped % each
    source = inner // RADIUS * token_cols + grouped // each * RADIUS + inner % RADIUS
    return (natural == source).astype(jnp.float32).astype(jnp.bfloat16)


def store_band(b, total, cells, stream, inputs):
    each = BAND * RADIUS
    units = each // inputs.shape[2]
    at = pl.ds(pl.multiple_of(b * each, each), each)
    for g in range(inputs.shape[0]):
        rows = slice(g * each, (g + 1) * each)
        stream[g, at, :] = total[rows]
        inputs[g, pl.ds(b * units, units)] = cells[rows].reshape(
            units, each // units, cells.shape[1]
        )


def merge_kernel(
    rows, token_cols, meta, got, weights, embed, gain, stream, inputs, num, den, turned
):
    tiles, _, lanes = got.shape
    capacity = meta.shape[0] // tiles
    num[...] = jnp.zeros_like(num)
    den[...] = jnp.ones_like(den)

    def add_tile(t, c):
        for r in range(capacity):
            m = meta[t * capacity + r]
            w = weights[m >> 8]
            at = pl.ds(pl.multiple_of((m & 255) * 8, 8), rows)
            num[at, :] += got[t, r * rows : (r + 1) * rows, :].astype(jnp.float32) * w
            den[at, :] += w
        return c

    lax.fori_loop(0, tiles, add_tile, 0)
    group = PATCH * 8

    def turn(i, c):
        at = pl.ds(pl.multiple_of(i * group, group), group)
        merged = (num[at, :] / den[at, :]).astype(jnp.bfloat16).astype(jnp.float32)
        turned[pl.ds(pl.multiple_of(i * lanes, lanes), lanes), :] = merged.T
        return c

    lax.fori_loop(0, TOK_H, turn, 0, unroll=4)
    part = BAND * token_cols
    order = regroup(token_cols)

    def embed_part(k, c):
        parts = [
            turned[pl.ds(k * part * PATCH + q, part, stride=PATCH), :] for q in range(PATCH)
        ]
        lhs = jnp.concatenate(parts, 1).astype(jnp.bfloat16)
        lhs = jnp.dot(order, lhs, preferred_element_type=jnp.float32).astype(jnp.bfloat16)
        total = jnp.dot(lhs, embed[...], preferred_element_type=jnp.float32)
        store_band(k, total, normed(total, gain[...]), stream, inputs)
        return c

    lax.fori_loop(0, TOK_H // BAND, embed_part, 0)


def layer_kernel(layer, last, token_cols, sizes, x, qkv, out_w, stream, bias, gain, *refs):
    outs, refs = (refs[:1], refs[1:]) if last else (refs[:2], refs[2:])
    q_ref, kv, w, wo, xh, w_sem, send, recv = refs
    width = wo.shape[0]
    head_dim = width // HEADS
    groups, units, unit, _ = x.shape
    own = units * unit
    count = groups * own
    loads = [
        pltpu.make_async_copy(
            qkv.at[layer, :, n * width : (n + 1) * width], w.at[n], w_sem.at[n]
        )
        for n in range(3)
    ] + [pltpu.make_async_copy(out_w.at[layer], wo, w_sem.at[3])]
    for load in loads:
        load.start()

    row, col = lax.axis_index("row"), lax.axis_index("col")
    up, down = row > 0, row < sizes[0] - 1
    west, east = col > 0, col < sizes[1] - 1
    top, bottom = xh.at[:groups], xh.at[groups : 2 * groups]
    l0 = 2 * groups
    r0 = l0 + units + 2
    end = r0 + units + 2
    moves = [
        (-1, 0, up, x.at[:, 0], bottom, top),
        (1, 0, down, x.at[:, units - 1], top, bottom),
        (0, -1, west, x.at[0], xh.at[r0 + 1 : end - 1], xh.at[l0 + 1 : r0 - 1]),
        (0, 1, east, x.at[groups - 1], xh.at[l0 + 1 : r0 - 1], xh.at[r0 + 1 : end - 1]),
        (-1, -1, up & west, x.at[0, 0], xh.at[end - 1], xh.at[l0]),
        (-1, 1, up & east, x.at[groups - 1, 0], xh.at[r0 - 1], xh.at[r0]),
        (1, -1, down & west, x.at[0, units - 1], xh.at[r0], xh.at[r0 - 1]),
        (1, 1, down & east, x.at[groups - 1, units - 1], xh.at[l0], xh.at[end - 1]),
    ]
    opposite = [1, 0, 3, 2, 7, 6, 5, 4]
    barrier = pltpu.get_barrier_semaphore()
    mesh_ids = pl.DeviceIdType.MESH
    for dr, dc, there, _, _, _ in moves:

        @pl.when(there)
        def _(dr=dr, dc=dc):
            pl.semaphore_signal(
                barrier, inc=1, device_id=(row + dr, col + dc), device_id_type=mesh_ids
            )

    for _, _, there, _, _, here in moves:

        @pl.when(jnp.logical_not(there))
        def _(here=here):
            here[...] = jnp.zeros(here.shape, here.dtype)

    rows_near = 1 + up.astype(jnp.int32) + down.astype(jnp.int32)
    cols_near = 1 + west.astype(jnp.int32) + east.astype(jnp.int32)
    pl.semaphore_wait(barrier, rows_near * cols_near - 1)
    copies = []
    for n, (dr, dc, there, source, lands, _) in enumerate(moves):
        copies.append(
            pltpu.make_async_remote_copy(
                src_ref=source,
                dst_ref=lands,
                send_sem=send.at[n],
                recv_sem=recv.at[n],
                device_id=(row + dr, col + dc),
                device_id_type=mesh_ids,
            )
        )

        @pl.when(there)
        def _(copy=copies[-1]):
            copy.start()

    step = 512

    def project(n, put):
        rows = x if n < 3 else xh
        weight = w.at[n] if n < 3 else w.at[n - 2]
        total = count if n < 3 else end * unit

        def part(k, c):
            cols = pl.ds(pl.multiple_of(k * step, step), step)
            y = jnp.dot(
                rows[...].reshape(total, width),
                weight[:, cols],
                preferred_element_type=jnp.float32,
            ).astype(jnp.bfloat16)
            put(k, y)
            return c

        lax.fori_loop(0, width // step, part, 0)

    def put_q(k, y):
        cols = pl.ds(pl.multiple_of(k * step, step), step)
        for g in range(groups):
            q_ref[g, :, cols] = (y[g * own : (g + 1) * own] * head_dim ** (-0.5)).astype(
                jnp.bfloat16
            )

    def put_own(base, k, y):
        cols = pl.ds(pl.multiple_of(base + k * step, step), step)
        for g in range(groups):
            kv[g + 1, unit : unit + own, cols] = y[g * own : (g + 1) * own]

    def put_halo(base, k, y):
        cols = pl.ds(pl.multiple_of(base + k * step, step), step)
        for g in range(groups):
            kv[g + 1, :unit, cols] = y[g * unit : (g + 1) * unit]
            kv[g + 1, unit + own :, cols] = y[(groups + g) * unit : (groups + g + 1) * unit]
        kv[0, :, cols] = y[l0 * unit : r0 * unit]
        kv[groups + 1, :, cols] = y[r0 * unit :]

    loads[0].wait()
    project(0, put_q)
    for n in (1, 2):
        loads[n].wait()
        project(n, functools.partial(put_own, (n - 1) * width))
    for n, (_, _, there, _, _, here) in enumerate(moves):

        @pl.when(there)
        def _(n=n, here=here):
            copies[n].wait_send()
            pltpu.make_async_remote_copy(
                src_ref=here,
                dst_ref=here,
                send_sem=send.at[n],
                recv_sem=recv.at[opposite[n]],
                device_id=(row + moves[n][0], col + moves[n][1]),
                device_id_type=mesh_ids,
            ).wait_recv()

    for n in (3, 4):
        project(n, functools.partial(put_halo, (n - 3) * width))
    loads[3].wait()
    each = BAND * RADIUS
    span = (BAND + 2 * RADIUS) * RADIUS
    pair = 2 * head_dim
    queries = 2 * each
    low = lax.broadcasted_iota(jnp.int32, (queries, pair), 1) < head_dim
    ones = jnp.ones((4 * span, pair), jnp.bfloat16)
    order = regroup(token_cols, True) if last else None

    def band(b, carry):
        q_at = pl.ds(pl.multiple_of(b * each, each), each)
        k_at = pl.ds(pl.multiple_of(b * each, each), span)
        halves = []
        for s in range(groups // 2):
            half_bias = bias[b, s]
            both = jnp.concatenate([half_bias, half_bias], 0)
            pieces = []
            for h in range(HEADS // 2):
                cols = slice(h * pair, (h + 1) * pair)
                v_cols = slice(width + h * pair, width + (h + 1) * pair)
                q = jnp.concatenate([q_ref[2 * s + i, q_at, cols] for i in range(2)], 0)
                zero = jnp.zeros_like(q)
                q2 = jnp.concatenate([jnp.where(low, q, zero), jnp.where(low, zero, q)], 0)
                k = jnp.concatenate([kv[2 * s + i, k_at, cols] for i in range(4)], 0)
                v = jnp.concatenate([kv[2 * s + i, k_at, v_cols] for i in range(4)], 0)
                logits = lax.dot_general(
                    q2, k, (((1,), (1,)), ((), ())), preferred_element_type=jnp.float32
                )
                logits = logits + both
                top_logit = jnp.max(logits, -1, keepdims=True)
                weight = jnp.exp(logits - top_logit).astype(jnp.bfloat16)
                summed = jnp.dot(
                    weight, jnp.concatenate([v, ones], 1), preferred_element_type=jnp.float32
                )
                share = summed[:, :pair] / summed[:, pair:]
                pieces.append(
                    jnp.where(low, share[:queries], share[queries:]).astype(jnp.bfloat16)
                )
            halves.append(jnp.concatenate(pieces, 1))
        attended = jnp.concatenate(halves, 0)
        before = jnp.concatenate([stream[g, q_at, :] for g in range(groups)], 0)
        total = before + jnp.dot(attended, wo[...], preferred_element_type=jnp.float32)
        if last:
            rows = BAND * token_cols
            outs[0][pl.ds(pl.multiple_of(b * rows, rows), rows), :] = jnp.dot(
                order, total.astype(jnp.bfloat16), preferred_element_type=jnp.float32
            ).astype(jnp.bfloat16)
        else:
            store_band(b, total, normed(total, gain[...]), outs[0], outs[1])
        return carry

    lax.fori_loop(0, TOK_H // BAND, band, 0)


def window_bias(token_cols):
    bands, halves = TOK_H // BAND, token_cols // (2 * RADIUS)
    win = BAND + 2 * RADIUS
    q = jnp.arange(2 * BAND * RADIUS, dtype=jnp.int32)
    k = jnp.arange(4 * win * RADIUS, dtype=jnp.int32)
    q_row = q % (BAND * RADIUS) // RADIUS
    q_col = q // (BAND * RADIUS) * RADIUS + q % RADIUS
    k_row = k % (win * RADIUS) // RADIUS - RADIUS
    k_col = k // (win * RADIUS) * RADIUS + k % RADIUS - RADIUS
    near = (jnp.abs(k_row[None] - q_row[:, None]) <= RADIUS) & (
        jnp.abs(k_col[None] - q_col[:, None]) <= RADIUS
    )
    g_row = (
        lax.axis_index("row") * TOK_H
        + jnp.arange(bands, dtype=jnp.int32)[:, None] * BAND
        + k_row[None]
    )
    g_col = (
        lax.axis_index("col") * token_cols
        + jnp.arange(halves, dtype=jnp.int32)[:, None] * 2 * RADIUS
        + k_col[None]
    )
    row_in = (g_row >= 0) & (g_row < TOK_H * lax.axis_size("row"))
    col_in = (g_col >= 0) & (g_col < token_cols * lax.axis_size("col"))
    inside = row_in[:, None] & col_in[None]
    return jnp.where(near[None, None] & inside[:, :, None], 0.0, -1e30).astype(jnp.float32)


def per_device(
    scans, dest, offsets, profile_index, profiles, embed_weight, attn_gain, qkv_weight, out_weight
):
    device_count = lax.axis_size("row") * lax.axis_size("col")
    blocks, strip_rows, channels, tile_cols = scans.shape
    token_cols = tile_cols // PATCH
    count = TOK_H * token_cols
    tile_rows = TOK_H * PATCH
    profile_count = profiles.shape[0]
    width = embed_weight.shape[1]
    layers = qkv_weight.shape[0]
    capacity = max(2, 2 * blocks // device_count)
    slots = device_count * capacity
    rows = strip_rows * channels
    extra = -(-capacity // 16) * 16
    f32, bf16 = jnp.float32, jnp.bfloat16
    params = pltpu.CompilerParams(vmem_limit_bytes=56 * 2**20)

    payload = pl.pallas_call(
        functools.partial(place_kernel, capacity),
        out_shape=jax.ShapeDtypeStruct((device_count, capacity * rows + extra, tile_cols), bf16),
        in_specs=[SMEM, SMEM, SMEM, VMEM],
        out_specs=VMEM,
        scratch_shapes=[
            pltpu.VMEM((device_count, extra, tile_cols), f32),
            pltpu.SMEM((device_count,), jnp.int32),
        ],
        compiler_params=params,
        name="place",
    )(dest[:, 0], offsets, profile_index, scans.reshape(blocks, rows, tile_cols))
    got = lax.all_to_all(payload, ("row", "col"), split_axis=0, concat_axis=0, tiled=True)
    named = got[:, capacity * rows : capacity * rows + capacity, :]
    meta = (named[:, :, 0] + named[:, :, tile_cols // 2].astype(f32) * 256.0).astype(jnp.int32)
    meta = meta.reshape(slots)
    weights = jnp.broadcast_to(
        profiles[:, :, None, :], (profile_count, strip_rows, channels, tile_cols)
    ).reshape(profile_count, rows, tile_cols)
    weights = jnp.concatenate([jnp.zeros((1, rows, tile_cols), f32), weights], 0)
    embed = (
        embed_weight.reshape(channels, PATCH, PATCH, width)
        .transpose(2, 1, 0, 3)
        .reshape(PATCH * PATCH * channels, width)
    )
    bias = window_bias(token_cols)
    groups = token_cols // RADIUS
    unit = RADIUS * RADIUS
    units = TOK_H // RADIUS
    state = (
        jax.ShapeDtypeStruct((groups, units * unit, width), f32),
        jax.ShapeDtypeStruct((groups, units, unit, width), bf16),
    )
    stream, inputs = pl.pallas_call(
        functools.partial(merge_kernel, rows, token_cols),
        out_shape=state,
        in_specs=[SMEM, VMEM, VMEM, VMEM, VMEM],
        out_specs=(VMEM,) * 2,
        scratch_shapes=[
            pltpu.VMEM((tile_rows * channels, tile_cols), f32),
            pltpu.VMEM((tile_rows * channels, tile_cols), f32),
            pltpu.VMEM((TOK_H * tile_cols, PATCH * channels), f32),
        ],
        compiler_params=params,
        name="merge",
    )(meta, got, weights, embed, attn_gain[:1])
    sizes = (lax.axis_size("row"), lax.axis_size("col"))
    hbm = pl.BlockSpec(memory_space=pl.ANY)
    for l in range(layers):
        last = l == layers - 1
        result = pl.pallas_call(
            functools.partial(layer_kernel, l, last, token_cols, sizes),
            out_shape=jax.ShapeDtypeStruct((count, width), bf16) if last else state,
            in_specs=[VMEM, hbm, hbm, VMEM, VMEM, VMEM],
            out_specs=VMEM if last else (VMEM,) * 2,
            scratch_shapes=[
                pltpu.VMEM((groups, units * unit, width), bf16),
                pltpu.VMEM((groups + 2, (units + 2) * unit, 2 * width), bf16),
                pltpu.VMEM((3, width, width), bf16),
                pltpu.VMEM((width, width), bf16),
                pltpu.VMEM((2 * groups + 2 * (units + 2), unit, width), bf16),
                pltpu.SemaphoreType.DMA((4,)),
                pltpu.SemaphoreType.DMA((8,)),
                pltpu.SemaphoreType.DMA((8,)),
            ],
            compiler_params=pltpu.CompilerParams(
                vmem_limit_bytes=56 * 2**20, collective_id=l, has_side_effects=True
            ),
            name="layer" + str(l),
        )(
            inputs,
            qkv_weight,
            out_weight,
            stream,
            bias,
            attn_gain[min(l + 1, layers - 1)][None],
        )
        if last:
            return result.reshape(TOK_H, token_cols, width)
        stream, inputs = result


def solution(mesh):
    placed = (
        P(("row", "col"), None, None, None),
        P(("row", "col"), None),
        P(("row", "col")),
        P(("row", "col")),
        P(),
        P(),
        P(),
        P(),
        P(),
    )
    return jax.shard_map(
        per_device, mesh=mesh, in_specs=placed, out_specs=P("row", "col", None), check_vma=False
    )
```
